512 devices in a mesh: var: 32 (over z_lo, y, core), head: 16 (over z_hi, x).
Axes of the slice: x: 4, y: 4, z: 16 (z_hi: 4, z_lo: 4; z = z_hi * 4 + z_lo), core: 2. Of those that a mesh axis runs over, the one named last changes fastest.
Arguments:
- queries: bfloat16 [16384, 8192], P('var', 'head'), may hold values from -5 to 5
- ablated: int32 [16384], P('var'), may hold values from 0 to 63
- head_keep: int32 [32, 64], P(None, 'head'), may hold values 0 or 1
- k_cache: bfloat16 [32, 2048, 1024], P('var', 'head'), may hold values from -4 to 4
- v_cache: bfloat16 [32, 2048, 1024], P('var', 'head'), may hold values from -40 to 40
- lengths: int32 [32], P('var'), may hold values from 512 to 2048, as said below
- out_weight: bfloat16 [8192, 4096], P('head', 'var'), may hold values from -0.125 to 0.125
- residual: bfloat16 [16384, 4096], P('var', 'head'), may hold values from -6 to 6
Outputs:
- patched: bfloat16 [16384, 4096], P('var', 'head')
The draws below stay inside these ranges and needn't reach their ends.
Inputs may be any that keep to these rules, and one draw needn't show every extreme that they name: `lengths`: one prompt has exactly 2048 live positions.
All inputs are finite; a program needn't handle non-finite values. No bound on the sum of `head_keep` on one device may be relied on, other than what follows from the above.
Results may differ from the reference program's by a relative error of at most 0.012.
Values may be sent and summed in bfloat16 or wider, within the bound.
No kernel may reach another device: no remote copies, remote signals or barrier semaphores. Data moves between devices by JAX's collectives and lax.ppermute only.
A program may use at most 64 MiB of HBM per device.

```python
import math
import jax
import jax.numpy as jnp
from jax import lax

HEADS = 64
KVH = 8
HD = 128
D_OUT = 4096
L = 2048
VROWS = 512
PROMPTS = 32
ROWS = 16384
N_VAR = 32
N_HEAD = 16


def draw_queries(key, part):
    result = jnp.clip(jax.random.normal(jax.random.fold_in(key, 1), (ROWS, HEADS, HD), jnp.float32), -5.0, 5.0)
    return result.reshape(ROWS, HEADS * HD).astype(jnp.bfloat16)


def draw_k_cache(key, part):
    result = jnp.clip(jax.random.normal(jax.random.fold_in(key, 2), (PROMPTS, L, KVH, HD), jnp.float32), -4.0, 4.0)
    return result.reshape(PROMPTS, L, KVH * HD).astype(jnp.bfloat16)


def draw_lengths(key, part):
    drawn = jax.random.randint(jax.random.fold_in(key, 4), (PROMPTS,), L // 4, L + 1)
    longest = jax.random.randint(jax.random.fold_in(key, 5), (), 0, PROMPTS)
    return jnp.where(jnp.arange(PROMPTS) == longest, L, drawn).astype(jnp.int32)


def plant(entries, stream_key, smallest, high):
    dims = entries.shape
    index_at = [jax.random.randint(jax.random.fold_in(stream_key, axis), (), 0, dims[axis]) for axis in range(len(dims))]
    entries = entries.at[tuple(index_at)].set(smallest)
    longest = dims.index(max(dims))
    index_at[longest] = (index_at[longest] + 1) % dims[longest]
    return entries.at[tuple(index_at)].set(high)


def raised(values, stream_key, source, target, blocks, factor):
    owner, partner = [(jnp.arange(values.shape[axis_at]) // (values.shape[axis_at] // blocks)).reshape([-1 if axis == axis_at else 1 for axis in range(values.ndim)]) for axis_at in (source, target)]
    chosen = jax.random.permutation(stream_key, blocks)[partner]
    strong = (owner == chosen) | (owner == (partner + blocks // 2) % blocks)
    return jnp.where(strong, factor * values, values)


def level_of(stream_key, extent, cuts, least, top_value):
    gain, own = 1.0, jax.random.fold_in(stream_key, 6)
    for axis_at, parts in cuts:
        heights = jnp.exp(jax.random.uniform(jax.random.fold_in(own, axis_at), (parts,), jnp.float32, least / len(cuts), top_value / len(cuts)))
        gain = gain * jnp.repeat(heights, extent[axis_at] // parts).reshape([-1 if axis == axis_at else 1 for axis in range(len(extent))])
    return gain


def centred(key, extent, scale, limit, shards=(), kind=jnp.bfloat16):
    entries = scale * jax.random.normal(key, extent, jnp.float32)
    if shards:
        entries = entries * level_of(key, extent, shards, -0.22, 0.18)
    return jnp.clip(entries, -limit, limit).astype(kind)


def gaussian_with(key, extent, scale, most, split, heavy, held_as=jnp.bfloat16):
    entries = scale * jax.random.normal(key, extent, jnp.float32)
    if split:
        entries = entries * level_of(key, extent, split, -0.22, 0.18)
    return jnp.clip(raised(entries, jax.random.fold_in(key, 3), *heavy), -most, most).astype(held_as)


def setup_inputs(seed: int = 0) -> dict:
    seeds = jax.random.split(jax.random.key(seed), 9)
    return {
        "queries": draw_queries(jax.random.fold_in(seeds[8], 71), 0),
        "ablated": plant(jax.random.randint(seeds[1], (ROWS,), 0, HEADS), jax.random.fold_in(seeds[1], 1), 0, HEADS - 1).astype(jnp.int32),
        "head_keep": plant((jax.random.randint(seeds[2], (PROMPTS, HEADS), 0, 8) < 7).astype(jnp.int32), jax.random.fold_in(seeds[2], 1), 0, 1),
        "k_cache": draw_k_cache(jax.random.fold_in(seeds[8], 71), 0),
        "v_cache": centred(seeds[4], (PROMPTS, L, KVH * HD), 8.0, 40.0, ((0, 32), (1, 16))),
        "lengths": draw_lengths(jax.random.fold_in(seeds[8], 71), 0),
        "out_weight": gaussian_with(seeds[6], (HEADS * HD, D_OUT), (HEADS * HD) ** -0.5, 0.125, ((0, 16), (1, 32)), (0, 1, 32, 2.75)),
        "residual": centred(seeds[7], (ROWS, D_OUT), 1.0, 6.0, ((0, 32), (1, 16))),
    }


def reference(queries, ablated, head_keep, k_cache, v_cache, lengths, out_weight, residual):
    per_prompt = VROWS // N_VAR
    group_size = HEADS // KVH
    local_heads = HEADS // N_HEAD
    score_scale = 1.0 / math.sqrt(HD)
    grouped = queries.reshape(N_VAR, PROMPTS, per_prompt, HEADS, HD).transpose(1, 0, 2, 3, 4)
    grouped = grouped.reshape(PROMPTS, VROWS, KVH, group_size, HD)

    def one_prompt(prompt_inputs):
        prompt_queries, prompt_keys, prompt_values, prompt_length = prompt_inputs
        prompt_keys = prompt_keys.reshape(L, KVH, HD)
        prompt_values = prompt_values.reshape(L, KVH, HD)
        scores = jnp.einsum('rkgd,tkd->kgrt', prompt_queries.astype(jnp.float32), prompt_keys.astype(jnp.float32)) * score_scale
        visible = jnp.arange(L) < prompt_length
        scores = jnp.where(visible, scores, -jnp.inf)
        row_max = lax.optimization_barrier(jnp.max(scores, axis=-1, keepdims=True))
        exponent = jnp.exp(scores - row_max)
        probs = (exponent / lax.optimization_barrier(jnp.sum(exponent, axis=-1, keepdims=True))).astype(jnp.bfloat16)
        outputs = jnp.einsum('kgrt,tkd->rkgd', probs.astype(jnp.float32), prompt_values.astype(jnp.float32)).astype(jnp.bfloat16)
        return outputs.reshape(VROWS, HEADS * HD)
    head_out = lax.map(one_prompt, (grouped, k_cache, v_cache, lengths))
    head_out = head_out.reshape(PROMPTS, N_VAR, per_prompt, HEADS * HD).transpose(1, 0, 2, 3).reshape(ROWS, HEADS * HD)
    prompt_of_row = (jnp.arange(ROWS) % VROWS // per_prompt).astype(jnp.int32)
    kept_rows = head_keep[prompt_of_row]
    kept_heads = jnp.where(ablated[:, None] != jnp.arange(HEADS)[None, :], kept_rows, 0)
    gated = (head_out.reshape(ROWS, HEADS, HD) * kept_heads[:, :, None].astype(jnp.bfloat16)).reshape(ROWS, HEADS * HD)
    summed = jnp.zeros((ROWS, D_OUT), jnp.float32)
    span = local_heads * HD
    for group_index in range(N_HEAD):
        partial_value = jnp.dot(gated[:, group_index * span:(group_index + 1) * span], out_weight[group_index * span:(group_index + 1) * span], preferred_element_type=jnp.float32).astype(jnp.bfloat16)
        summed = summed + partial_value.astype(jnp.float32)
    projected = summed.astype(jnp.bfloat16)
    return (residual.astype(jnp.float32) + projected.astype(jnp.float32)).astype(jnp.bfloat16)
```

```python
import functools
import math

import jax
import jax.numpy as jnp
from jax import lax
from jax.experimental import pallas as pl
from jax.experimental.pallas import tpu as pltpu
from jax.sharding import Mesh, PartitionSpec as P

HEADS = 64
KVH = 8
HD = 128
VAR = ("zl", "y", "c")
HEAD = ("zh", "x")
ROW_BLOCK = 128


def attend_kernel(info, q_ref, kv_ref, ab_ref, out_ref, k_all, v_all):
    xs, zs, _, span, _ = kv_ref.shape

    @pl.when(pl.program_id(0) == 0)
    def _():
        for z in range(zs):
            for x in range(xs):
                at = pl.ds((z * xs + x) * span, span)
                k_all[at, :] = kv_ref[x, z, 0]
                v_all[at, :] = kv_ref[x, z, 1]

    positions = k_all.shape[0]
    live = lax.broadcasted_iota(jnp.int32, (1, positions), 1) < info[0]
    bias = jnp.where(live, 0.0, -jnp.inf).astype(jnp.float32)
    scale = math.log2(math.e) / math.sqrt(HD)
    for j in range(q_ref.shape[1] // HD):
        cols = slice(j * HD, (j + 1) * HD)
        scores = lax.dot_general(
            q_ref[:, cols], k_all[...], (((1,), (1,)), ((), ())), preferred_element_type=jnp.float32
        )
        scores = scores * scale + bias
        top = jnp.max(scores, axis=-1, keepdims=True)
        weight = jnp.exp2(scores - top)
        total = jnp.sum(weight, axis=-1, keepdims=True)
        mixed = jnp.dot(weight.astype(jnp.bfloat16), v_all[...], preferred_element_type=jnp.float32)
        keep = jnp.logical_and(ab_ref[...] != info[1] + j, info[2 + j] != 0)
        out_ref[:, cols] = jnp.where(keep, mixed / total, 0.0).astype(jnp.bfloat16)


def attend(info, queries, kv, ablated):
    rows, feats = queries.shape
    xs, zs, _, span, _ = kv.shape
    positions = xs * zs * span
    heads = feats // HD
    return pl.pallas_call(
        attend_kernel,
        out_shape=jax.ShapeDtypeStruct((rows, feats), jnp.bfloat16),
        grid_spec=pltpu.PrefetchScalarGridSpec(
            num_scalar_prefetch=1,
            grid=(rows // ROW_BLOCK,),
            in_specs=[
                pl.BlockSpec((ROW_BLOCK, feats), lambda i, s: (i, 0)),
                pl.BlockSpec(kv.shape, lambda i, s: (0, 0, 0, 0, 0)),
                pl.BlockSpec((ROW_BLOCK, 1), lambda i, s: (i, 0)),
            ],
            out_specs=pl.BlockSpec((ROW_BLOCK, feats), lambda i, s: (i, 0)),
            scratch_shapes=[
                pltpu.VMEM((positions, HD), jnp.bfloat16),
                pltpu.VMEM((positions, HD), jnp.bfloat16),
            ],
        ),
        cost_estimate=pl.CostEstimate(
            flops=4 * rows * feats * positions,
            transcendentals=rows * heads * positions,
            bytes_accessed=4 * rows * feats + 2 * kv.size,
        ),
        compiler_params=pltpu.CompilerParams(vmem_limit_bytes=40 << 20),
        name="attend",
    )(info, queries, kv, ablated)


def place_kernel(where, *refs):
    parts, out_ref = refs[:-1], refs[-1]
    for t, part in enumerate(parts):
        for s in range(4):
            for j in range(4):
                x = where[8 + t * 4 + j]
                k0 = pl.multiple_of(where[t] * 128, 128)
                n0 = pl.multiple_of(where[4 + s] * 128, 128)
                out_ref[x, pl.ds(k0, 128), pl.ds(n0, 128)] = part[s, j]


def place(where, parts):
    n = len(parts)
    spec = pl.BlockSpec(memory_space=pltpu.VMEM)
    return pl.pallas_call(
        place_kernel,
        out_shape=jax.ShapeDtypeStruct((4, 512, 512), jnp.bfloat16),
        in_specs=[pl.BlockSpec(memory_space=pltpu.SMEM)] + [spec] * n,
        out_specs=spec,
        cost_estimate=pl.CostEstimate(flops=0, transcendentals=0, bytes_accessed=4 << 20),
        compiler_params=pltpu.CompilerParams(vmem_limit_bytes=16 << 20),
        name="place",
    )(where, *parts)


def project_kernel(core, g_ref, own_ref, other_ref, out_ref):
    c = core[0]
    parts = g_ref.shape[0]
    for u, w_ref in enumerate((own_ref, other_ref)):
        lanes = pl.ds(pl.multiple_of((c if u == 0 else 1 - c) * 128, 128), 128)
        for pair in range(2):
            total = None
            for x in range(parts):
                term = jnp.dot(
                    g_ref[x], w_ref[x, :, pair * 256 : (pair + 1) * 256], preferred_element_type=jnp.float32
                )
                total = term if total is None else total + term
            total = total.astype(jnp.bfloat16)
            out_ref[2 * pair, :, lanes] = total[:, :128]
            out_ref[2 * pair + 1, :, lanes] = total[:, 128:]


def project(core, gated, own, other):
    parts, rows, feats = gated.shape
    spec = pl.BlockSpec(memory_space=pltpu.VMEM)
    return pl.pallas_call(
        project_kernel,
        out_shape=jax.ShapeDtypeStruct((4, rows, 256), jnp.bfloat16),
        in_specs=[pl.BlockSpec(memory_space=pltpu.SMEM)] + [spec] * 3,
        out_specs=spec,
        cost_estimate=pl.CostEstimate(
            flops=2 * parts * rows * feats * 1024, transcendentals=0, bytes_accessed=8 << 20
        ),
        compiler_params=pltpu.CompilerParams(vmem_limit_bytes=24 << 20),
        name="project",
    )(core, gated, own, other)


def shifted(size, by):
    return [(i, (i + by) % size) for i in range(size)]


def gather_weight(out_weight):
    y = lax.axis_index("y")
    x = lax.axis_index("x")
    zl = lax.axis_index("zl")
    pieces = out_weight.reshape(4, 128, 128)
    crossed = []
    for j in range(4):
        piece = lax.dynamic_index_in_dim(pieces, (x + j) % 4, 0, keepdims=False)
        pairs = [(sy * 4 + sx, ((sx + j) % 4) * 4 + sy) for sy in range(4) for sx in range(4)]
        crossed.append(lax.ppermute(piece, ("y", "x"), pairs))
    mine = jnp.stack(crossed)
    along = jnp.stack([mine] + [lax.ppermute(mine, "zl", shifted(4, s)) for s in (1, 2, 3)])
    parts = [along] + [lax.ppermute(along, "y", shifted(4, t)) for t in (1, 2, 3)]
    rows_of = [(y - t) % 4 for t in range(4)]
    cols_of = [(zl - s) % 4 for s in range(4)]
    x_of = [(rows_of[t] - j) % 4 for t in range(4) for j in range(4)]
    own = place(jnp.stack(rows_of + cols_of + x_of).astype(jnp.int32), parts)
    other = lax.ppermute(own, "c", [(0, 1), (1, 0)])
    return own, other


def per_device(queries, ablated, head_keep, k_cache, v_cache, lengths, out_weight, residual):
    row_count, feature_count = queries.shape
    prompts, local_heads = head_keep.shape
    per_prompt = row_count // prompts
    span = k_cache.shape[1]
    var_position = lax.axis_index(VAR)
    head_position = lax.axis_index(HEAD)

    kv = jnp.stack([k_cache[0], v_cache[0]]).reshape(2, span, 4, 2 * HD).transpose(2, 0, 1, 3)
    kv = lax.all_to_all(kv, "zh", 0, 0, tiled=True)
    kv = jnp.stack([kv[..., :HD], kv[..., :HD], kv[..., HD:], kv[..., HD:]])
    kv = lax.all_to_all(kv, "x", 0, 0, tiled=True)

    own, other = gather_weight(out_weight)

    arrived = lax.all_to_all(
        queries.reshape(prompts, per_prompt, feature_count), VAR, 0, 0, tiled=True
    ).reshape(row_count, feature_count)
    ablated_here = lax.all_to_all(ablated.reshape(prompts, per_prompt), VAR, 0, 0, tiled=True)

    keep = lax.dynamic_index_in_dim(head_keep, var_position, 0, keepdims=False)
    info = jnp.concatenate([lengths, (head_position * local_heads)[None].astype(jnp.int32), keep])
    gated = attend(info, arrived, kv, ablated_here.reshape(row_count, 1))

    gathered = lax.all_to_all(
        jnp.broadcast_to(gated[None], (4, row_count, feature_count)), "x", 0, 0, tiled=True
    )
    partial = project(lax.axis_index("c")[None].astype(jnp.int32), gathered, own, other)
    partial = partial.reshape(4 * prompts, per_prompt, 256)
    returned = lax.all_to_all(partial, ("zh",) + VAR, 0, 0, tiled=True)
    projected = jnp.sum(returned.reshape(4, row_count, 256).astype(jnp.float32), axis=0)
    projected = projected.astype(jnp.bfloat16)
    return (residual.astype(jnp.float32) + projected.astype(jnp.float32)).astype(jnp.bfloat16)


def solution(mesh):
    split = Mesh(mesh.devices.reshape(4, 4, 2, 4, 4), VAR + HEAD)
    return jax.shard_map(
        per_device,
        mesh=split,
        in_specs=(
            P(VAR, HEAD),
            P(VAR),
            P(None, HEAD),
            P(VAR, HEAD, None),
            P(VAR, HEAD, None),
            P(VAR),
            P(HEAD, VAR),
            P(VAR, HEAD),
        ),
        out_specs=P(VAR, HEAD),
        check_vma=False,
    )
```

```python
import math

import jax
import jax.numpy as jnp
from jax import lax
from jax.experimental import pallas as pl
from jax.experimental.pallas import tpu as pltpu
from jax.sharding import Mesh, PartitionSpec as P


HD = 128
VAR = ("zl", "y", "c")
HEAD = ("zh", "x")
ROW_BLOCK = 128


def attend_kernel(info, q_ref, *refs):
    kv, (out_ref, k_all, v_all) = refs[:-3], refs[-3:]
    slots, _, span, _ = kv[0].shape
    base = 1 + q_ref.shape[1] // HD

    @pl.when(pl.program_id(0) == 0)
    def _():
        for t, kv_ref in enumerate(kv):
            for s in range(slots):
                at = pl.ds(pl.multiple_of(info[base + t * slots + s] * span, span), span)
                k_all[at, :] = kv_ref[s, 0]
                v_all[at, :] = kv_ref[s, 1]

    positions = k_all.shape[0]
    live = lax.broadcasted_iota(jnp.int32, (1, positions), 1) < info[0]
    bias = jnp.where(live, 0.0, -jnp.inf).astype(jnp.float32)
    scale = math.log2(math.e) / math.sqrt(HD)
    for j in range(q_ref.shape[1] // HD):
        cols = slice(j * HD, (j + 1) * HD)
        scores = lax.dot_general(
            q_ref[:, cols], k_all[...], (((1,), (1,)), ((), ())), preferred_element_type=jnp.float32
        )
        scores = scores * scale + bias
        top = jnp.max(scores, axis=-1, keepdims=True)
        weight = jnp.exp2(scores - top)
        total = jnp.sum(weight, axis=-1, keepdims=True)
        mixed = jnp.dot(weight.astype(jnp.bfloat16), v_all[...], preferred_element_type=jnp.float32)
        first = q_ref[:, j * HD : j * HD + 1].astype(jnp.float32)
        keep = jnp.logical_and(first != jnp.inf, info[1 + j] != 0)
        out_ref[:, cols] = jnp.where(keep, mixed / total, 0.0).astype(jnp.bfloat16)


def attend(info, queries, kv):
    rows, feats = queries.shape
    slots, _, span, _ = kv[0].shape
    positions = len(kv) * slots * span
    return pl.pallas_call(
        attend_kernel,
        out_shape=jax.ShapeDtypeStruct((rows, feats), jnp.bfloat16),
        grid_spec=pltpu.PrefetchScalarGridSpec(
            num_scalar_prefetch=1,
            grid=(rows // ROW_BLOCK,),
            in_specs=[pl.BlockSpec((ROW_BLOCK, feats), lambda i, s: (i, 0))]
            + [pl.BlockSpec(kv[0].shape, lambda i, s: (0, 0, 0, 0))] * len(kv),
            out_specs=pl.BlockSpec((ROW_BLOCK, feats), lambda i, s: (i, 0)),
            scratch_shapes=[
                pltpu.VMEM((positions, HD), jnp.bfloat16),
                pltpu.VMEM((positions, HD), jnp.bfloat16),
            ],
        ),
        cost_estimate=pl.CostEstimate(
            flops=4 * rows * feats * positions,
            transcendentals=rows * (feats // HD) * positions,
            bytes_accessed=4 * rows * feats + 4 * positions * HD,
        ),
        compiler_params=pltpu.CompilerParams(vmem_limit_bytes=40 << 20),
        name="attend",
    )(info, queries, *kv)


def place_kernel(where, *refs):
    parts, out_ref = refs[:-1], refs[-1]
    for t, part in enumerate(parts):
        for s in range(4):
            out_ref[where[t], :, pl.ds(pl.multiple_of(where[4 + s] * 128, 128), 128)] = part[s]


def place(where, parts):
    spec = pl.BlockSpec(memory_space=pltpu.VMEM)
    return pl.pallas_call(
        place_kernel,
        out_shape=jax.ShapeDtypeStruct((4, 512, 512), jnp.bfloat16),
        in_specs=[pl.BlockSpec(memory_space=pltpu.SMEM)] + [spec] * len(parts),
        out_specs=spec,
        cost_estimate=pl.CostEstimate(flops=0, transcendentals=0, bytes_accessed=4 << 20),
        compiler_params=pltpu.CompilerParams(vmem_limit_bytes=16 << 20),
        name="place",
    )(where, *parts)


def project_kernel(where, *refs):
    gated, (own_ref, other_ref, out_ref) = refs[:-3], refs[-3:]
    c = where[0]
    for u, w_ref in enumerate((own_ref, other_ref)):
        lanes = pl.ds(pl.multiple_of((c if u == 0 else 1 - c) * 128, 128), 128)
        for pair in range(2):
            total = None
            for s, g_ref in enumerate(gated):
                term = jnp.dot(
                    g_ref[...],
                    w_ref[where[1 + s], :, pair * 256 : (pair + 1) * 256],
                    preferred_element_type=jnp.float32,
                )
                total = term if total is None else total + term
            total = total.astype(jnp.bfloat16)
            out_ref[2 * pair, :, lanes] = total[:, :128]
            out_ref[2 * pair + 1, :, lanes] = total[:, 128:]


def project(where, gated, own, other):
    parts = len(gated)
    rows, feats = gated[0].shape
    spec = pl.BlockSpec(memory_space=pltpu.VMEM)
    return pl.pallas_call(
        project_kernel,
        out_shape=jax.ShapeDtypeStruct((4, rows, 256), jnp.bfloat16),
        in_specs=[pl.BlockSpec(memory_space=pltpu.SMEM)] + [spec] * (parts + 2),
        out_specs=spec,
        cost_estimate=pl.CostEstimate(
            flops=2 * parts * rows * feats * 1024, transcendentals=0, bytes_accessed=8 << 20
        ),
        compiler_params=pltpu.CompilerParams(vmem_limit_bytes=24 << 20),
        name="project",
    )(where, *gated, own, other)


def shifted(size, by):
    return [(i, (i + by) % size) for i in range(size)]


def gather_weight(out_weight, y, zl):
    turned = lax.ppermute(out_weight, ("y", "x"), [(y * 4 + x, x * 4 + y) for y in range(4) for x in range(4)])
    along = [turned]
    for s in (1, 2, 3):
        along.append(lax.ppermute(turned, "zl", shifted(4, s)))
    along = jnp.stack(along)
    parts = [along]
    for s in (1, 2, 3):
        parts.append(lax.ppermute(along, "y", shifted(4, s)))
    where = jnp.stack([(y + 4 - t) & 3 for t in range(4)] + [(zl + 4 - s) & 3 for s in range(4)])
    own = place(where.astype(jnp.int32), parts)
    other = lax.ppermute(own, "c", [(0, 1), (1, 0)])
    return own, other


def step(queries, ablated, head_keep, k_cache, v_cache, lengths, out_weight, residual):
    row_count, feature_count = queries.shape
    prompts, local_heads = head_keep.shape
    per_prompt = row_count // prompts
    var_position = lax.axis_index(VAR)
    head_position = lax.axis_index(HEAD)
    x = lax.axis_index("x")
    first_head = head_position * local_heads

    zh = lax.axis_index("zh")
    caches = jnp.stack([k_cache[0], v_cache[0]])

    def heads_for(other_zh):
        return lax.dynamic_slice_in_dim(caches, other_zh * (2 * HD), 2 * HD, 2)

    kv = [heads_for(zh)]
    for s in (1, 2, 3):
        kv.append(lax.ppermute(heads_for((zh + s) & 3), "zh", shifted(4, s)))
    kv = jnp.stack(kv)

    def head_for(other_x):
        return lax.dynamic_slice_in_dim(kv, (other_x >> 1) * HD, HD, 3)

    kv_here = [head_for(x)]
    for t in (1, 2, 3):
        kv_here.append(lax.ppermute(head_for((x + t) & 3), "x", shifted(4, t)))
    block_of = [((zh - s) & 3) * 4 + ((x - t) & 3) for t in range(4) for s in range(4)]

    own, other = gather_weight(out_weight, lax.axis_index("y"), lax.axis_index("zl"))

    head_of = first_head + lax.broadcasted_iota(jnp.int32, (1, feature_count), 1) // HD
    marked = jnp.where(ablated[:, None] == head_of, jnp.inf, queries).astype(queries.dtype)
    arrived = lax.all_to_all(
        marked.reshape(prompts, per_prompt, feature_count), VAR, 0, 0, tiled=True
    ).reshape(row_count, feature_count)

    keep = lax.dynamic_index_in_dim(head_keep, var_position, 0, keepdims=False)
    gated = attend(jnp.concatenate([lengths, keep, jnp.stack(block_of)]), arrived, kv_here)

    gathered = [gated]
    for s in (1, 2, 3):
        gathered.append(lax.ppermute(gated, "x", shifted(4, s)))
    where = jnp.stack([lax.axis_index("c")] + [(x + 4 - s) & 3 for s in range(4)]).astype(jnp.int32)
    partial = project(where, gathered, own, other)
    partial = partial.reshape(4 * prompts, per_prompt, 256)
    returned = lax.all_to_all(partial, ("zh",) + VAR, 0, 0, tiled=True)
    projected = jnp.sum(returned.reshape(4, row_count, 256).astype(jnp.float32), axis=0)
    projected = projected.astype(jnp.bfloat16)
    return (residual.astype(jnp.float32) + projected.astype(jnp.float32)).astype(jnp.bfloat16)


def solution(mesh):
    split = Mesh(mesh.devices.reshape(4, 4, 2, 4, 4), VAR + HEAD)
    return jax.shard_map(
        step,
        mesh=split,
        in_specs=(
            P(VAR, HEAD),
            P(VAR),
            P(None, HEAD),
            P(VAR, HEAD, None),
            P(VAR, HEAD, None),
            P(VAR),
            P(HEAD, VAR),
            P(VAR, HEAD),
        ),
        out_specs=P(VAR, HEAD),
        check_vma=False,
    )
```

```python
import math

import jax
import jax.numpy as jnp
from jax import lax
from jax.experimental import pallas as pl
from jax.experimental.pallas import tpu as pltpu
from jax.sharding import Mesh, PartitionSpec as P


HD = 128
VAR = ("zl", "y", "c")
HEAD = ("zh", "x")
ROW_BLOCK = 256
DEAD = -1e30


def attend_kernel(info, q_ref, *refs):
    kv, (out_ref, k_all, v_all) = refs[:-3], refs[-3:]
    slots, _, span, _ = kv[0].shape
    rows, feats = q_ref.shape
    heads = feats // HD
    base = 1 + heads

    @pl.when(pl.program_id(0) == 0)
    def _():
        for t, kv_ref in enumerate(kv):
            for s in range(slots):
                first = pl.multiple_of(info[base + t * slots + s] * span, span)
                at = pl.ds(first, span)
                position = first + lax.broadcasted_iota(jnp.int32, (span, HD), 0)
                k_all[at, :HD] = kv_ref[s, 0]
                k_all[at, HD:] = jnp.where(position < info[0], 0.0, DEAD).astype(jnp.bfloat16)
                v_all[at, :HD] = kv_ref[s, 1]
                v_all[at, HD:] = jnp.ones((span, HD), jnp.bfloat16)

    scale = math.log2(math.e) / math.sqrt(HD)
    one = (lax.broadcasted_iota(jnp.int32, (rows, HD), 1) == 0).astype(jnp.bfloat16)

    def scores_of(j):
        query = jnp.concatenate([q_ref[:, j * HD : (j + 1) * HD], one], axis=1)
        return lax.dot_general(
            query, k_all[...], (((1,), (1,)), ((), ())), preferred_element_type=jnp.float32
        )

    scores = scores_of(0)
    for j in range(heads):
        following = scores_of(j + 1) if j + 1 < heads else None
        top = jnp.max(scores, axis=-1, keepdims=True)
        weight = jnp.exp2((scores - top) * scale).astype(jnp.bfloat16)
        mixed = jnp.dot(weight, v_all[...], preferred_element_type=jnp.float32)
        mixed = mixed[:, :HD] / mixed[:, HD : HD + 1]
        mark = q_ref[:, j * HD : j * HD + 1].astype(jnp.float32)
        keep = jnp.logical_and(mark != jnp.inf, info[1 + j] != 0)
        out_ref[:, j * HD : (j + 1) * HD] = jnp.where(keep, mixed, 0.0).astype(jnp.bfloat16)
        scores = following


def attend(info, queries, kv):
    rows, feats = queries.shape
    slots, _, span, _ = kv[0].shape
    positions = len(kv) * slots * span
    return pl.pallas_call(
        attend_kernel,
        out_shape=jax.ShapeDtypeStruct((rows, feats), jnp.bfloat16),
        grid_spec=pltpu.PrefetchScalarGridSpec(
            num_scalar_prefetch=1,
            grid=(rows // ROW_BLOCK,),
            in_specs=[pl.BlockSpec((ROW_BLOCK, feats), lambda i, s: (i, 0))]
            + [pl.BlockSpec(kv[0].shape, lambda i, s: (0, 0, 0, 0))] * len(kv),
            out_specs=pl.BlockSpec((ROW_BLOCK, feats), lambda i, s: (i, 0)),
            scratch_shapes=[
                pltpu.VMEM((positions, 2 * HD), jnp.bfloat16),
                pltpu.VMEM((positions, 2 * HD), jnp.bfloat16),
            ],
        ),
        cost_estimate=pl.CostEstimate(
            flops=4 * rows * feats * positions,
            transcendentals=rows * (feats // HD) * positions,
            bytes_accessed=4 * rows * feats + 4 * positions * HD,
        ),
        compiler_params=pltpu.CompilerParams(vmem_limit_bytes=24 << 20),
        name="attend",
    )(info, queries, *kv)


def place_kernel(where, *refs):
    parts, (out_ref, held, sems) = refs[:-3], refs[-3:]
    copies = [pltpu.make_async_copy(part, held.at[t], sems.at[t]) for t, part in enumerate(parts)]
    for copy in copies:
        copy.start()
    for t, copy in enumerate(copies):
        copy.wait()
        for s in range(4):
            out_ref[where[t], :, pl.ds(pl.multiple_of(where[4 + s] * 128, 128), 128)] = held[t, s]


def place(where, parts):
    return pl.pallas_call(
        place_kernel,
        out_shape=jax.ShapeDtypeStruct((4, 512, 512), jnp.bfloat16),
        in_specs=[pl.BlockSpec(memory_space=pltpu.SMEM)] + [pl.BlockSpec(memory_space=pl.ANY)] * len(parts),
        out_specs=pl.BlockSpec(memory_space=pltpu.VMEM),
        scratch_shapes=[
            pltpu.VMEM((len(parts), 4, 512, 128), jnp.bfloat16),
            pltpu.SemaphoreType.DMA((len(parts),)),
        ],
        cost_estimate=pl.CostEstimate(flops=0, transcendentals=0, bytes_accessed=4 << 20),
        name="place",
    )(where, *parts)


def project_kernel(where, *refs):
    gated, (own_ref, other_any, out_ref, other_ref, sem) = refs[:-5], refs[-5:]
    fetch = pltpu.make_async_copy(other_any, other_ref, sem)
    fetch.start()
    c = where[0]
    rows = jnp.concatenate([g_ref[...] for g_ref in gated], axis=1)
    for u, w_ref in enumerate((own_ref, other_ref)):
        if u == 1:
            fetch.wait()
        lanes = pl.ds(pl.multiple_of((c if u == 0 else 1 - c) * 128, 128), 128)
        for pair in range(2):
            weight = [w_ref[where[1 + s], :, pair * 256 : (pair + 1) * 256] for s in range(len(gated))]
            total = jnp.dot(
                rows, jnp.concatenate(weight, axis=0), preferred_element_type=jnp.float32
            ).astype(jnp.bfloat16)
            out_ref[2 * pair, :, lanes] = total[:, :128]
            out_ref[2 * pair + 1, :, lanes] = total[:, 128:]


def project(where, gated, own, other):
    parts = len(gated)
    rows, feats = gated[0].shape
    spec = pl.BlockSpec(memory_space=pltpu.VMEM)
    return pl.pallas_call(
        project_kernel,
        out_shape=jax.ShapeDtypeStruct((4, rows, 256), jnp.bfloat16),
        in_specs=[pl.BlockSpec(memory_space=pltpu.SMEM)]
        + [spec] * (parts + 1)
        + [pl.BlockSpec(memory_space=pl.ANY)],
        out_specs=spec,
        scratch_shapes=[pltpu.VMEM(other.shape, other.dtype), pltpu.SemaphoreType.DMA],
        cost_estimate=pl.CostEstimate(
            flops=2 * parts * rows * feats * 1024, transcendentals=0, bytes_accessed=8 << 20
        ),
        compiler_params=pltpu.CompilerParams(vmem_limit_bytes=16 << 20),
        name="project",
    )(where, *gated, own, other)


def shifted(size, by):
    return [(i, (i + by) % size) for i in range(size)]


def gather_weight(out_weight, y, zl):
    turned = lax.ppermute(out_weight, ("y", "x"), [(y * 4 + x, x * 4 + y) for y in range(4) for x in range(4)])
    pair = jnp.stack([turned, lax.ppermute(turned, "zl", [(i, i ^ 1) for i in range(4)])])
    far = lax.ppermute(pair, "zl", [(i, i ^ 2) for i in range(4)])
    along = jnp.concatenate([pair, far])
    parts = [along]
    for s in (1, 2, 3):
        parts.append(lax.ppermute(along, "y", shifted(4, s)))
    where = jnp.stack([(y + 4 - t) & 3 for t in range(4)] + [zl ^ s for s in range(4)])
    own = place(where.astype(jnp.int32), parts)
    other = lax.ppermute(own, "c", [(0, 1), (1, 0)])
    return own, other


def step(queries, ablated, head_keep, k_cache, v_cache, lengths, out_weight, residual):
    row_count, feature_count = queries.shape
    prompts, local_heads = head_keep.shape
    per_prompt = row_count // prompts
    var_position = lax.axis_index(VAR)
    head_position = lax.axis_index(HEAD)
    x = lax.axis_index("x")
    first_head = head_position * local_heads

    zh = lax.axis_index("zh")

    def heads_for(other_zh):
        first = other_zh * (2 * HD)
        return jnp.stack([lax.dynamic_slice_in_dim(c[0], first, 2 * HD, 1) for c in (k_cache, v_cache)])

    kv = [heads_for(zh)]
    for s in (1, 2, 3):
        kv.append(lax.ppermute(heads_for((zh + s) & 3), "zh", shifted(4, s)))
    kv = jnp.stack(kv)

    def head_for(other_x):
        return lax.dynamic_slice_in_dim(kv, (other_x >> 1) * HD, HD, 3)

    kv_here = [head_for(x)]
    for t in (1, 2, 3):
        kv_here.append(lax.ppermute(head_for((x + t) & 3), "x", shifted(4, t)))
    block_of = [((zh - s) & 3) * 4 + ((x - t) & 3) for t in range(4) for s in range(4)]

    own, other = gather_weight(out_weight, lax.axis_index("y"), lax.axis_index("zl"))

    head_of = first_head + lax.broadcasted_iota(jnp.int32, (1, feature_count), 1) // HD
    marked = jnp.where(ablated[:, None] == head_of, jnp.inf, queries).astype(queries.dtype)
    arrived = lax.all_to_all(
        marked.reshape(prompts, per_prompt, feature_count), VAR, 0, 0, tiled=True
    ).reshape(row_count, feature_count)

    keep = lax.dynamic_index_in_dim(head_keep, var_position, 0, keepdims=False)
    gated = attend(jnp.concatenate([lengths, keep, jnp.stack(block_of)]), arrived, kv_here)

    gathered = [gated]
    for s in (1, 2, 3):
        gathered.append(lax.ppermute(gated, "x", shifted(4, s)))
    where = jnp.stack([lax.axis_index("c")] + [(x + 4 - s) & 3 for s in range(4)]).astype(jnp.int32)
    partial = project(where, gathered, own, other)
    partial = partial.reshape(4 * prompts, per_prompt, 256)
    returned = lax.all_to_all(partial, ("zh",) + VAR, 0, 0, tiled=True)
    projected = jnp.sum(returned.reshape(4, row_count, 256).astype(jnp.float32), axis=0)
    projected = projected.astype(jnp.bfloat16)
    return (residual.astype(jnp.float32) + projected.astype(jnp.float32)).astype(jnp.bfloat16)


def solution(mesh):
    split = Mesh(mesh.devices.reshape(4, 4, 2, 4, 4), VAR + HEAD)
    return jax.shard_map(
        step,
        mesh=split,
        in_specs=(
            P(VAR, HEAD),
            P(VAR),
            P(None, HEAD),
            P(VAR, HEAD, None),
            P(VAR, HEAD, None),
            P(VAR),
            P(HEAD, VAR),
            P(VAR, HEAD),
        ),
        out_specs=P(VAR, HEAD),
        check_vma=False,
    )
```

```python
import math

import jax
import jax.numpy as jnp
from jax import lax
from jax.experimental import pallas as pl
from jax.experimental.pallas import tpu as pltpu
from jax.sharding import Mesh, PartitionSpec as P


HD = 128
VAR = ("zl", "y", "c")
HEAD = ("zh", "x")
ROW_BLOCK = 256
DEAD = -1e30


def attend_kernel(info, q_ref, *refs):
    kv, (out_ref, k_all, v_all) = refs[:-3], refs[-3:]
    slots, _, span, _ = kv[0].shape
    rows, feats = q_ref.shape
    heads = feats // HD
    base = 1 + heads

    @pl.when(pl.program_id(0) == 0)
    def _():
        for t, kv_ref in enumerate(kv):
            for s in range(slots):
                first = pl.multiple_of(info[base + t * slots + s] * span, span)
                at = pl.ds(first, span)
                position = first + lax.broadcasted_iota(jnp.int32, (span, HD), 0)
                k_all[at, :HD] = kv_ref[s, 0]
                k_all[at, HD:] = jnp.where(position < info[0], 0.0, DEAD).astype(jnp.bfloat16)
                v_all[at, :HD] = kv_ref[s, 1]
                v_all[at, HD:] = jnp.ones((span, HD), jnp.bfloat16)

    scale = math.log2(math.e) / math.sqrt(HD)
    one = (lax.broadcasted_iota(jnp.int32, (rows, HD), 1) == 0).astype(jnp.bfloat16)

    def scores_of(j):
        query = jnp.concatenate([q_ref[:, j * HD : (j + 1) * HD], one], axis=1)
        return lax.dot_general(
            query, k_all[...], (((1,), (1,)), ((), ())), preferred_element_type=jnp.float32
        )

    scores = scores_of(0)
    for j in range(heads):
        following = scores_of(j + 1) if j + 1 < heads else None
        top = jnp.max(scores, axis=-1, keepdims=True)
        weight = jnp.exp2((scores - top) * scale).astype(jnp.bfloat16)
        mixed = jnp.dot(weight, v_all[...], preferred_element_type=jnp.float32)
        mixed = mixed[:, :HD] / mixed[:, HD : HD + 1]
        mark = q_ref[:, j * HD : j * HD + 1].astype(jnp.float32)
        keep = jnp.logical_and(mark != jnp.inf, info[1 + j] != 0)
        out_ref[:, j * HD : (j + 1) * HD] = jnp.where(keep, mixed, 0.0).astype(jnp.bfloat16)
        scores = following


def attend(info, queries, kv):
    rows, feats = queries.shape
    slots, _, span, _ = kv[0].shape
    positions = len(kv) * slots * span
    return pl.pallas_call(
        attend_kernel,
        out_shape=jax.ShapeDtypeStruct((rows, feats), jnp.bfloat16),
        grid_spec=pltpu.PrefetchScalarGridSpec(
            num_scalar_prefetch=1,
            grid=(rows // ROW_BLOCK,),
            in_specs=[pl.BlockSpec((ROW_BLOCK, feats), lambda i, s: (i, 0))]
            + [pl.BlockSpec(kv[0].shape, lambda i, s: (0, 0, 0, 0))] * len(kv),
            out_specs=pl.BlockSpec((ROW_BLOCK, feats), lambda i, s: (i, 0)),
            scratch_shapes=[
                pltpu.VMEM((positions, 2 * HD), jnp.bfloat16),
                pltpu.VMEM((positions, 2 * HD), jnp.bfloat16),
            ],
        ),
        cost_estimate=pl.CostEstimate(
            flops=4 * rows * feats * positions,
            transcendentals=rows * (feats // HD) * positions,
            bytes_accessed=4 * rows * feats + 4 * positions * HD,
        ),
        compiler_params=pltpu.CompilerParams(vmem_limit_bytes=24 << 20),
        name="attend",
    )(info, queries, *kv)


def project_kernel(where, *refs):
    gated, (own_ref, other_any, out_ref, other_ref, sem) = refs[:-5], refs[-5:]
    fetch = pltpu.make_async_copy(other_any, other_ref, sem)
    fetch.start()
    c = where[0]
    rows = jnp.concatenate([g_ref[...] for g_ref in gated], axis=1)
    for u, w_ref in enumerate((own_ref, other_ref)):
        if u == 1:
            fetch.wait()
        lanes = pl.ds(pl.multiple_of((c if u == 0 else 1 - c) * 128, 128), 128)
        for pair in (0, 2):
            weight = jnp.concatenate(
                [
                    jnp.concatenate([w_ref[where[1 + s], pair], w_ref[where[1 + s], pair + 1]], axis=1)
                    for s in range(len(gated))
                ],
                axis=0,
            )
            total = jnp.dot(rows, weight, preferred_element_type=jnp.float32).astype(jnp.bfloat16)
            out_ref[where[1 + len(gated)] ^ pair, :, lanes] = total[:, :128]
            out_ref[where[1 + len(gated)] ^ (pair + 1), :, lanes] = total[:, 128:]


def project(where, gated, own, other):
    parts = len(gated)
    rows, feats = gated[0].shape
    spec = pl.BlockSpec(memory_space=pltpu.VMEM)
    return pl.pallas_call(
        project_kernel,
        out_shape=jax.ShapeDtypeStruct((4, rows, 256), jnp.bfloat16),
        in_specs=[pl.BlockSpec(memory_space=pltpu.SMEM)]
        + [spec] * (parts + 1)
        + [pl.BlockSpec(memory_space=pltpu.HBM)],
        out_specs=spec,
        scratch_shapes=[pltpu.VMEM(other.shape, other.dtype), pltpu.SemaphoreType.DMA],
        cost_estimate=pl.CostEstimate(
            flops=2 * parts * rows * feats * 1024, transcendentals=0, bytes_accessed=8 << 20
        ),
        compiler_params=pltpu.CompilerParams(vmem_limit_bytes=16 << 20),
        name="project",
    )(where, *gated, own, other)


def shifted(size, by):
    return [(i, (i + by) % size) for i in range(size)]


def gather_weight(out_weight):
    turned = lax.ppermute(out_weight, ("y", "x"), [(y * 4 + x, x * 4 + y) for y in range(4) for x in range(4)])
    pair = jnp.stack([turned, lax.ppermute(turned, "zl", [(i, i ^ 1) for i in range(4)])])
    far = lax.ppermute(pair, "zl", [(i, i ^ 2) for i in range(4)])
    along = jnp.concatenate([pair, far])
    own = lax.all_to_all(jnp.broadcast_to(along[None], (4,) + along.shape), "y", 0, 0, tiled=True)
    other = lax.ppermute(own, "c", [(0, 1), (1, 0)])
    return own, other


def step(queries, ablated, head_keep, k_cache, v_cache, lengths, out_weight, residual):
    row_count, feature_count = queries.shape
    prompts, local_heads = head_keep.shape
    per_prompt = row_count // prompts
    var_position = lax.axis_index(VAR)
    head_position = lax.axis_index(HEAD)
    x = lax.axis_index("x")
    first_head = head_position * local_heads

    zh = lax.axis_index("zh")

    def heads_for(other_zh):
        first = other_zh * (2 * HD)
        return jnp.stack([lax.dynamic_slice_in_dim(c[0], first, 2 * HD, 1) for c in (k_cache, v_cache)])

    kv = [heads_for(zh)]
    for s in (1, 2, 3):
        kv.append(lax.ppermute(heads_for((zh + s) & 3), "zh", shifted(4, s)))
    kv = jnp.stack(kv)

    def head_for(other_x):
        return lax.dynamic_slice_in_dim(kv, (other_x >> 1) * HD, HD, 3)

    kv_here = [head_for(x)]
    for t in (1, 2, 3):
        kv_here.append(lax.ppermute(head_for((x + t) & 3), "x", shifted(4, t)))
    block_of = [((zh - s) & 3) * 4 + ((x - t) & 3) for t in range(4) for s in range(4)]

    own, other = gather_weight(out_weight)

    head_of = first_head + lax.broadcasted_iota(jnp.int32, (1, feature_count), 1) // HD
    marked = jnp.where(ablated[:, None] == head_of, jnp.inf, queries).astype(queries.dtype)
    arrived = lax.all_to_all(
        marked.reshape(prompts, per_prompt, feature_count), VAR, 0, 0, tiled=True
    ).reshape(row_count, feature_count)

    keep = lax.dynamic_index_in_dim(head_keep, var_position, 0, keepdims=False)
    gated = attend(jnp.concatenate([lengths, keep, jnp.stack(block_of)]), arrived, kv_here)

    gathered = [gated]
    for s in (1, 2, 3):
        gathered.append(lax.ppermute(gated, "x", shifted(4, s)))
    where = [lax.axis_index("c")] + [(x + 4 - s) & 3 for s in range(4)] + [lax.axis_index("zl")]
    where = jnp.stack(where).astype(jnp.int32)
    partial = project(where, gathered, own, other)
    partial = partial.reshape(4 * prompts, per_prompt, 256)
    returned = lax.all_to_all(partial, ("zh",) + VAR, 0, 0, tiled=True)
    projected = jnp.sum(returned.reshape(4, row_count, 256).astype(jnp.float32), axis=0)
    projected = projected.astype(jnp.bfloat16)
    return (residual.astype(jnp.float32) + projected.astype(jnp.float32)).astype(jnp.bfloat16)


def solution(mesh):
    split = Mesh(mesh.devices.reshape(4, 4, 2, 4, 4), VAR + HEAD)
    return jax.shard_map(
        step,
        mesh=split,
        in_specs=(
            P(VAR, HEAD),
            P(VAR),
            P(None, HEAD),
            P(VAR, HEAD, None),
            P(VAR, HEAD, None),
            P(VAR),
            P(HEAD, VAR),
            P(VAR, HEAD),
        ),
        out_specs=P(VAR, HEAD),
        check_vma=False,
    )
```

```python
import math

import jax
import jax.numpy as jnp
from jax import lax
from jax.experimental import pallas as pl
from jax.experimental.pallas import tpu as pltpu
from jax.sharding import Mesh, PartitionSpec as P


HD = 128
VAR = ("zl", "y", "c")
HEAD = ("zh", "x")
ROW_BLOCK = 256
DEAD = -1e30


def attend_kernel(info, q_ref, *refs):
    kv, (out_ref, k_all, v_all) = refs[:-3], refs[-3:]
    slots, _, span, _ = kv[0].shape
    rows, feats = q_ref.shape
    heads = feats // HD
    base = 1 + heads

    @pl.when(pl.program_id(0) == 0)
    def _():
        for t, kv_ref in enumerate(kv):
            for s in range(slots):
                first = pl.multiple_of(info[base + t * slots + s] * span, span)
                at = pl.ds(first, span)
                position = first + lax.broadcasted_iota(jnp.int32, (span, HD), 0)
                k_all[at, :HD] = kv_ref[s, 0]
                k_all[at, HD:] = jnp.where(position < info[0], 0.0, DEAD).astype(jnp.bfloat16)
                v_all[at, :HD] = kv_ref[s, 1]
                v_all[at, HD:] = jnp.ones((span, HD), jnp.bfloat16)

    scale = math.log2(math.e) / math.sqrt(HD)
    one = (lax.broadcasted_iota(jnp.int32, (rows, HD), 1) == 0).astype(jnp.bfloat16)

    def scores_of(j):
        query = jnp.concatenate([q_ref[:, j * HD : (j + 1) * HD], one], axis=1)
        return lax.dot_general(
            query, k_all[...], (((1,), (1,)), ((), ())), preferred_element_type=jnp.float32
        )

    scores = scores_of(0)
    for j in range(heads):
        following = scores_of(j + 1) if j + 1 < heads else None
        top = jnp.max(scores, axis=-1, keepdims=True)
        weight = jnp.exp2((scores - top) * scale).astype(jnp.bfloat16)
        mixed = jnp.dot(weight, v_all[...], preferred_element_type=jnp.float32)
        mixed = mixed[:, :HD] / mixed[:, HD : HD + 1]
        mark = q_ref[:, j * HD : j * HD + 1].astype(jnp.float32)
        keep = jnp.logical_and(mark != jnp.inf, info[1 + j] != 0)
        out_ref[:, j * HD : (j + 1) * HD] = jnp.where(keep, mixed, 0.0).astype(jnp.bfloat16)
        scores = following


def attend(info, queries, kv):
    rows, feats = queries.shape
    slots, _, span, _ = kv[0].shape
    positions = len(kv) * slots * span
    return pl.pallas_call(
        attend_kernel,
        out_shape=jax.ShapeDtypeStruct((rows, feats), jnp.bfloat16),
        grid_spec=pltpu.PrefetchScalarGridSpec(
            num_scalar_prefetch=1,
            grid=(rows // ROW_BLOCK,),
            in_specs=[pl.BlockSpec((ROW_BLOCK, feats), lambda i, s: (i, 0))]
            + [pl.BlockSpec(kv[0].shape, lambda i, s: (0, 0, 0, 0))] * len(kv),
            out_specs=pl.BlockSpec((ROW_BLOCK, feats), lambda i, s: (i, 0)),
            scratch_shapes=[
                pltpu.VMEM((positions, 2 * HD), jnp.bfloat16),
                pltpu.VMEM((positions, 2 * HD), jnp.bfloat16),
            ],
        ),
        cost_estimate=pl.CostEstimate(
            flops=4 * rows * feats * positions,
            transcendentals=rows * (feats // HD) * positions,
            bytes_accessed=4 * rows * feats + 4 * positions * HD,
        ),
        compiler_params=pltpu.CompilerParams(vmem_limit_bytes=24 << 20),
        name="attend",
    )(info, queries, *kv)


def project_kernel(where, *refs):
    gated, (own_ref, other_any, out_ref, other_ref, sem) = refs[:-5], refs[-5:]
    fetch = pltpu.make_async_copy(other_any, other_ref, sem)
    fetch.start()
    c = where[0]
    rows = jnp.concatenate([g_ref[...] for g_ref in gated], axis=1)
    for u, w_ref in enumerate((own_ref, other_ref)):
        if u == 1:
            fetch.wait()
        lanes = pl.ds(pl.multiple_of((c if u == 0 else 1 - c) * 128, 128), 128)
        for pair in (0, 2):
            weight = jnp.concatenate(
                [
                    jnp.concatenate([w_ref[where[1 + s], pair], w_ref[where[1 + s], pair + 1]], axis=1)
                    for s in range(len(gated))
                ],
                axis=0,
            )
            total = jnp.dot(rows, weight, preferred_element_type=jnp.float32).astype(jnp.bfloat16)
            out_ref[where[1 + len(gated)] ^ pair, :, lanes] = total[:, :128]
            out_ref[where[1 + len(gated)] ^ (pair + 1), :, lanes] = total[:, 128:]


def project(where, gated, own, other):
    parts = len(gated)
    rows, feats = gated[0].shape
    spec = pl.BlockSpec(memory_space=pltpu.VMEM)
    return pl.pallas_call(
        project_kernel,
        out_shape=jax.ShapeDtypeStruct((4, rows, 256), jnp.bfloat16),
        in_specs=[pl.BlockSpec(memory_space=pltpu.SMEM)]
        + [spec] * (parts + 1)
        + [pl.BlockSpec(memory_space=pltpu.HBM)],
        out_specs=spec,
        scratch_shapes=[pltpu.VMEM(other.shape, other.dtype), pltpu.SemaphoreType.DMA],
        cost_estimate=pl.CostEstimate(
            flops=2 * parts * rows * feats * 1024, transcendentals=0, bytes_accessed=8 << 20
        ),
        compiler_params=pltpu.CompilerParams(vmem_limit_bytes=16 << 20),
        name="project",
    )(where, *gated, own, other)


def shifted(size, by):
    return [(i, (i + by) % size) for i in range(size)]


def gather_weight(out_weight):
    turned = lax.ppermute(out_weight, ("y", "x"), [(y * 4 + x, x * 4 + y) for y in range(4) for x in range(4)])
    pair = jnp.stack([turned, lax.ppermute(turned, "zl", [(i, i ^ 1) for i in range(4)])])
    far = lax.ppermute(pair, "zl", [(i, i ^ 2) for i in range(4)])
    along = jnp.concatenate([pair, far])
    own = lax.all_to_all(jnp.broadcast_to(along[None], (4,) + along.shape), "y", 0, 0, tiled=True)
    other = lax.ppermute(own, "c", [(0, 1), (1, 0)])
    return own, other


def step(queries, ablated, head_keep, k_cache, v_cache, lengths, out_weight, residual):
    row_count, feature_count = queries.shape
    prompts, local_heads = head_keep.shape
    per_prompt = row_count // prompts
    var_position = lax.axis_index(VAR)
    head_position = lax.axis_index(HEAD)
    x = lax.axis_index("x")
    first_head = head_position * local_heads

    zh = lax.axis_index("zh")

    def heads_for(other_zh):
        first = other_zh * (2 * HD)
        return jnp.stack([lax.dynamic_slice_in_dim(c[0], first, 2 * HD, 1) for c in (k_cache, v_cache)])

    kv = [heads_for(zh)]
    for s in (1, 2, 3):
        kv.append(lax.ppermute(heads_for((zh + s) & 3), "zh", shifted(4, s)))
    kv = jnp.stack(kv)

    def head_for(other_x):
        return lax.dynamic_slice_in_dim(kv, (other_x >> 1) * HD, HD, 3)

    kv_here = [head_for(x)]
    for t in (1, 2, 3):
        kv_here.append(lax.ppermute(head_for((x + t) & 3), "x", shifted(4, t)))
    block_of = [((zh - s) & 3) * 4 + ((x - t) & 3) for t in range(4) for s in range(4)]

    own, other = gather_weight(out_weight)

    head_of = first_head + lax.broadcasted_iota(jnp.int32, (1, feature_count), 1) // HD
    marked = jnp.where(ablated[:, None] == head_of, jnp.inf, queries).astype(queries.dtype)
    rows = marked.reshape(4, prompts // 4, per_prompt, feature_count).transpose(1, 0, 2, 3)
    arrived = lax.all_to_all(
        rows.reshape(prompts, per_prompt, feature_count), ("y", "c", "zl"), 0, 0, tiled=True
    ).reshape(row_count, feature_count)

    keep = lax.dynamic_index_in_dim(head_keep, var_position, 0, keepdims=False)
    gated = attend(jnp.concatenate([lengths, keep, jnp.stack(block_of)]), arrived, kv_here)

    gathered = [gated]
    for s in (1, 2, 3):
        gathered.append(lax.ppermute(gated, "x", shifted(4, s)))
    where = [lax.axis_index("c")] + [(x + 4 - s) & 3 for s in range(4)] + [lax.axis_index("zl")]
    where = jnp.stack(where).astype(jnp.int32)
    partial = project(where, gathered, own, other)
    partial = partial.reshape(4 * prompts, per_prompt, 256)
    returned = lax.all_to_all(partial, ("zh", "y", "c", "zl"), 0, 0, tiled=True)
    projected = jnp.sum(returned.reshape(4, row_count, 256).astype(jnp.float32), axis=0)
    projected = projected.astype(jnp.bfloat16).reshape(prompts // 4, 4, per_prompt, 256)
    projected = projected.transpose(1, 0, 2, 3).reshape(row_count, 256)
    return (residual.astype(jnp.float32) + projected.astype(jnp.float32)).astype(jnp.bfloat16)


def solution(mesh):
    split = Mesh(mesh.devices.reshape(4, 4, 2, 4, 4), VAR + HEAD)
    return jax.shard_map(
        step,
        mesh=split,
        in_specs=(
            P(VAR, HEAD),
            P(VAR),
            P(None, HEAD),
            P(VAR, HEAD, None),
            P(VAR, HEAD, None),
            P(VAR),
            P(HEAD, VAR),
            P(VAR, HEAD),
        ),
        out_specs=P(VAR, HEAD),
        check_vma=False,
    )
```

```python
import math

import jax
import jax.numpy as jnp
from jax import lax
from jax.experimental import pallas as pl
from jax.experimental.pallas import tpu as pltpu
from jax.sharding import Mesh, PartitionSpec as P


HD = 128
VAR = ("zl", "y", "c")
HEAD = ("zh", "x")
ROW_BLOCK = 256
DEAD = -1e30


def attend_kernel(info, q_ref, *refs):
    kv, (out_ref, k_all, v_all) = refs[:-3], refs[-3:]
    slots, _, span, _ = kv[0].shape
    rows, feats = q_ref.shape
    heads = feats // HD
    base = 1 + heads

    @pl.when(pl.program_id(0) == 0)
    def _():
        for t, kv_ref in enumerate(kv):
            for s in range(slots):
                first = pl.multiple_of(info[base + t * slots + s] * span, span)
                at = pl.ds(first, span)
                position = first + lax.broadcasted_iota(jnp.int32, (span, HD), 0)
                k_all[at, :HD] = kv_ref[s, 0]
                k_all[at, HD:] = jnp.where(position < info[0], 0.0, DEAD).astype(jnp.bfloat16)
                v_all[at, :HD] = kv_ref[s, 1]
                v_all[at, HD:] = jnp.ones((span, HD), jnp.bfloat16)

    scale = math.log2(math.e) / math.sqrt(HD)
    one = (lax.broadcasted_iota(jnp.int32, (rows, HD), 1) == 0).astype(jnp.bfloat16)

    def scores_of(j):
        query = jnp.concatenate([q_ref[:, j * HD : (j + 1) * HD], one], axis=1)
        return lax.dot_general(
            query, k_all[...], (((1,), (1,)), ((), ())), preferred_element_type=jnp.float32
        )

    scores = scores_of(0)
    for j in range(heads):
        following = scores_of(j + 1) if j + 1 < heads else None
        top = jnp.max(scores, axis=-1, keepdims=True)
        weight = jnp.exp2((scores - top) * scale).astype(jnp.bfloat16)
        mixed = jnp.dot(weight, v_all[...], preferred_element_type=jnp.float32)
        mixed = mixed[:, :HD] / mixed[:, HD : HD + 1]
        mark = q_ref[:, j * HD : j * HD + 1].astype(jnp.float32)
        keep = jnp.logical_and(mark != jnp.inf, info[1 + j] != 0)
        out_ref[:, j * HD : (j + 1) * HD] = jnp.where(keep, mixed, 0.0).astype(jnp.bfloat16)
        scores = following


def attend(info, queries, kv):
    rows, feats = queries.shape
    slots, _, span, _ = kv[0].shape
    positions = len(kv) * slots * span
    return pl.pallas_call(
        attend_kernel,
        out_shape=jax.ShapeDtypeStruct((rows, feats), jnp.bfloat16),
        grid_spec=pltpu.PrefetchScalarGridSpec(
            num_scalar_prefetch=1,
            grid=(rows // ROW_BLOCK,),
            in_specs=[pl.BlockSpec((ROW_BLOCK, feats), lambda i, s: (i, 0))]
            + [pl.BlockSpec(kv[0].shape, lambda i, s: (0, 0, 0, 0))] * len(kv),
            out_specs=pl.BlockSpec((ROW_BLOCK, feats), lambda i, s: (i, 0)),
            scratch_shapes=[
                pltpu.VMEM((positions, 2 * HD), jnp.bfloat16),
                pltpu.VMEM((positions, 2 * HD), jnp.bfloat16),
            ],
        ),
        cost_estimate=pl.CostEstimate(
            flops=4 * rows * feats * positions,
            transcendentals=rows * (feats // HD) * positions,
            bytes_accessed=4 * rows * feats + 4 * positions * HD,
        ),
        compiler_params=pltpu.CompilerParams(vmem_limit_bytes=24 << 20),
        name="attend",
    )(info, queries, *kv)


def project_kernel(where, *refs):
    gated, (own_ref, other_any, out_ref, other_ref, sem) = refs[:-5], refs[-5:]
    fetch = pltpu.make_async_copy(other_any, other_ref, sem)
    fetch.start()
    c = where[0]
    rows = jnp.concatenate([g_ref[...] for g_ref in gated], axis=1)
    for u, w_ref in enumerate((own_ref, other_ref)):
        if u == 1:
            fetch.wait()
        lanes = pl.ds(pl.multiple_of((c if u == 0 else 1 - c) * 128, 128), 128)
        for pair in (0, 2):
            weight = jnp.concatenate(
                [
                    jnp.concatenate([w_ref[where[1 + s], pair], w_ref[where[1 + s], pair + 1]], axis=1)
                    for s in range(len(gated))
                ],
                axis=0,
            )
            total = jnp.dot(rows, weight, preferred_element_type=jnp.float32).astype(jnp.bfloat16)
            out_ref[where[1 + len(gated)] ^ pair, :, lanes] = total[:, :128]
            out_ref[where[1 + len(gated)] ^ (pair + 1), :, lanes] = total[:, 128:]


def project(where, gated, own, other):
    parts = len(gated)
    rows, feats = gated[0].shape
    spec = pl.BlockSpec(memory_space=pltpu.VMEM)
    return pl.pallas_call(
        project_kernel,
        out_shape=jax.ShapeDtypeStruct((4, rows, 256), jnp.bfloat16),
        in_specs=[pl.BlockSpec(memory_space=pltpu.SMEM)]
        + [spec] * (parts + 1)
        + [pl.BlockSpec(memory_space=pltpu.HBM)],
        out_specs=spec,
        scratch_shapes=[pltpu.VMEM(other.shape, other.dtype), pltpu.SemaphoreType.DMA],
        cost_estimate=pl.CostEstimate(
            flops=2 * parts * rows * feats * 1024, transcendentals=0, bytes_accessed=8 << 20
        ),
        compiler_params=pltpu.CompilerParams(vmem_limit_bytes=16 << 20),
        name="project",
    )(where, *gated, own, other)


def shifted(size, by):
    return [(i, (i + by) % size) for i in range(size)]


def gather_weight(out_weight):
    turned = lax.ppermute(out_weight, ("y", "x"), [(y * 4 + x, x * 4 + y) for y in range(4) for x in range(4)])
    pair = jnp.stack([turned, lax.ppermute(turned, "zl", [(i, i ^ 1) for i in range(4)])])
    far = lax.ppermute(pair, "zl", [(i, i ^ 2) for i in range(4)])
    along = jnp.concatenate([pair, far])
    own = lax.all_to_all(jnp.broadcast_to(along[None], (4,) + along.shape), "y", 0, 0, tiled=True)
    other = lax.ppermute(own, "c", [(0, 1), (1, 0)])
    return own, other


def step(queries, ablated, head_keep, k_cache, v_cache, lengths, out_weight, residual):
    row_count, feature_count = queries.shape
    prompts, local_heads = head_keep.shape
    per_prompt = row_count // prompts
    var_position = lax.axis_index(VAR)
    head_position = lax.axis_index(HEAD)
    x = lax.axis_index("x")
    first_head = head_position * local_heads

    zh = lax.axis_index("zh")

    def heads_for(other_zh):
        first = other_zh * (2 * HD)
        return jnp.stack([lax.dynamic_slice_in_dim(c[0], first, 2 * HD, 1) for c in (k_cache, v_cache)])

    kv = [heads_for(zh)]
    for s in (1, 2, 3):
        kv.append(lax.ppermute(heads_for((zh + s) & 3), "zh", shifted(4, s)))
    kv = jnp.stack(kv)

    def head_for(other_x):
        return lax.dynamic_slice_in_dim(kv, (other_x >> 1) * HD, HD, 3)

    kv_here = [head_for(x)]
    for t in (1, 2, 3):
        kv_here.append(lax.ppermute(head_for((x + t) & 3), "x", shifted(4, t)))
    block_of = [((zh - s) & 3) * 4 + ((x - t) & 3) for t in range(4) for s in range(4)]

    own, other = gather_weight(out_weight)

    head_of = first_head + lax.broadcasted_iota(jnp.int32, (1, feature_count), 1) // HD
    marked = jnp.where(ablated[:, None] == head_of, jnp.inf, queries).astype(queries.dtype)
    rows = marked.reshape(4, prompts // 4, per_prompt, feature_count).transpose(1, 0, 2, 3)
    arrived = lax.all_to_all(
        rows.reshape(prompts, per_prompt, feature_count), ("y", "c", "zl"), 0, 0, tiled=True
    ).reshape(row_count, feature_count)

    keep = lax.dynamic_index_in_dim(head_keep, var_position, 0, keepdims=False)
    gated = attend(jnp.concatenate([lengths, keep, jnp.stack(block_of)]), arrived, kv_here)

    gathered = [gated]
    for s in (1, 2, 3):
        gathered.append(lax.ppermute(gated, "x", shifted(4, s)))
    where = [lax.axis_index("c")] + [(x + 4 - s) & 3 for s in range(4)] + [lax.axis_index("zl")]
    where = jnp.stack(where).astype(jnp.int32)
    partial = project(where, gathered, own, other)
    partial = partial.reshape(4 * prompts, per_prompt, 256)
    returned = lax.all_to_all(partial, ("zh", "y", "c", "zl"), 0, 0, tiled=True)
    returned = returned.reshape(4, prompts // 4, 4, per_prompt, 256).astype(jnp.float32)
    projected = jnp.sum(returned, axis=0).astype(jnp.bfloat16).astype(jnp.float32)
    before = residual.reshape(4, prompts // 4, per_prompt, 256).astype(jnp.float32)
    patched = [(before[z] + projected[:, z]).astype(jnp.bfloat16) for z in range(4)]
    return jnp.concatenate(patched, axis=0).reshape(row_count, 256)


def solution(mesh):
    split = Mesh(mesh.devices.reshape(4, 4, 2, 4, 4), VAR + HEAD)
    return jax.shard_map(
        step,
        mesh=split,
        in_specs=(
            P(VAR, HEAD),
            P(VAR),
            P(None, HEAD),
            P(VAR, HEAD, None),
            P(VAR, HEAD, None),
            P(VAR),
            P(HEAD, VAR),
            P(VAR, HEAD),
        ),
        out_specs=P(VAR, HEAD),
        check_vma=False,
    )
```
